256 devices in a mesh: dom: 8 (over y, core), shard: 32 (over x, z).
Axes of the slice: x: 4, y: 4, z: 8, core: 2. Of those that a mesh axis runs over, the one named last changes fastest.
Arguments:
- features: bfloat16 [65536, 512], P(('dom', 'shard')), may hold values from -6 to 6
- w_self: bfloat16 [512, 512], replicated, may hold values from -0.25 to 0.25
- w_neigh: bfloat16 [512, 512], replicated, may hold values from -0.25 to 0.25
- cotangent: bfloat16 [65536, 512], P(('dom', 'shard')), may hold values from -6 to 6
- neighbours: int32 [65536, 32], P(('dom', 'shard')), may hold values from 0 to 640, as said below
- hub_slots: int32 [256], P(('dom', 'shard')), may hold values from 0 to 255, as said below
- send_rows: int32 [256, 32, 4], P(('dom', 'shard')), may hold values from 0 to 255, as said below
- send_counts: int32 [256, 32], P(('dom', 'shard')), may hold values from 1 to 4, as said below
Outputs:
- hidden: bfloat16 [65536, 512], P(('dom', 'shard'))
- grad_features: float32 [65536, 512], P(('dom', 'shard'))
- grad_self: float32 [512, 512], replicated
- grad_neigh: float32 [512, 512], replicated
The draws below stay inside these ranges and needn't reach their ends.
Inputs may be any that keep to these rules, and one draw needn't show every extreme that they name: `neighbours`: padding slots (640) come after a vertex's live slots; each vertex has 4 to 32 live slots. A slot at or above 512 names peer p and position k with k below send_counts of that peer for this device. Hub indices are skewed: some hubs are read far more than others. `hub_slots`: the 1 entries of one device are distinct local rows. `send_rows`: rows may repeat; entries at or past a peer's count are not live. `send_counts`: in every partition group one shard index receives 4 rows from every peer.
All inputs are finite; a program needn't handle non-finite values.
Results may differ from the reference program's by a relative error of at most 0.0052.
Values may be sent and summed in bfloat16 or wider, within the bound.
No kernel may reach another device: no remote copies, remote signals or barrier semaphores. Data moves between devices by JAX's collectives and lax.ppermute only.
A program may use at most 64 MiB of HBM per device.

```python
import jax
import jax.numpy as jnp
from jax import lax

F = 512
V_DEV = 256
DEG = 32
HUB_DEV = 1
CAP = 4
HUBS = 256
TOTAL_V = 65536
TABLE = 640
N_DOM = 8
N_SHARD = 32


def count_table(key):
    base_key, target_key = jax.random.split(jax.random.fold_in(key, 11))
    senders = N_DOM * N_SHARD
    base = jax.random.randint(base_key, (senders, N_SHARD), 1, CAP + 1)
    target = jax.random.randint(target_key, (N_DOM,), 0, N_SHARD)
    dom_of = jnp.arange(senders) // N_SHARD
    full = jnp.arange(N_SHARD)[None, :] == target[dom_of][:, None]
    return jnp.where(full, CAP, base).astype(jnp.int32)


def draw_send_counts(key, part):
    return count_table(key)


def draw_send_rows(key, part):
    return jax.random.randint(jax.random.fold_in(key, 23), (N_DOM * N_SHARD, N_SHARD, CAP), 0, V_DEV).astype(jnp.int32)


def draw_hub_slots(key, part):
    stride = V_DEV // HUB_DEV
    within = jnp.arange(HUBS) % HUB_DEV
    jitter = jax.random.randint(jax.random.fold_in(key, 31), (HUBS,), 0, stride)
    return (within * stride + jitter).astype(jnp.int32)


def draw_neighbours(key, part):
    total = V_DEV * N_DOM * N_SHARD
    counts = count_table(key)
    keys = jax.random.split(jax.random.fold_in(key, 47), 9)
    shape = (total, DEG)
    degree = jax.random.randint(keys[0], (total, 1), 4, DEG + 1)
    kind = jax.random.randint(keys[1], shape, 0, 10)
    local = jax.random.randint(keys[2], shape, 0, V_DEV)
    offset = jax.random.randint(keys[3], (), 0, HUBS)
    favour = (offset + jax.random.randint(keys[4], shape, 0, 16) * max(1, HUBS // 16)) % HUBS
    spread = jax.random.randint(keys[5], shape, 0, HUBS)
    coin = jax.random.randint(keys[6], shape, 0, 2)
    hub = jnp.where(coin == 0, favour, spread) + V_DEV
    peer = jax.random.randint(keys[7], shape, 0, N_SHARD)
    device = jnp.arange(total) // V_DEV
    group = device // N_SHARD
    place = device % N_SHARD
    sender = group[:, None] * N_SHARD + peer
    limit = counts[sender, place[:, None]]
    within = jax.random.randint(keys[8], shape, 0, 1 << 20) % limit
    bound = V_DEV + HUBS + peer * CAP + within
    value = jnp.where(kind < 4, local, jnp.where(kind < 7, hub, bound))
    slot = jnp.arange(DEG)[None, :]
    return jnp.where(slot < degree, value, TABLE).astype(jnp.int32)


def shard_levels(stream_key, extent, cuts, smallest, top_value):
    def one(position, shards_of):
        draws = jax.random.uniform(jax.random.fold_in(jax.random.fold_in(stream_key, 6), position), (shards_of,), jnp.float32, smallest / len(cuts), top_value / len(cuts))
        return jnp.repeat(jnp.exp(draws), extent[position] // shards_of).reshape((-1,) + (1,) * (len(extent) - position - 1))

    gain = one(*cuts[0])
    for cut in cuts[1:]:
        gain = gain * one(*cut)
    return gain


def noise(own_key, shape, scale, most, cuts=(), kind=jnp.bfloat16):
    entries = scale * jax.random.normal(own_key, shape, jnp.float32)
    if cuts:
        entries = entries * shard_levels(own_key, shape, cuts, -0.22, 0.18)
    return jnp.clip(entries, -most, most).astype(kind)


def setup_inputs(seed: int = 0) -> dict:
    key_of = jax.random.split(jax.random.key(seed), 9)
    features = noise(key_of[0], (TOTAL_V, F), 1.0, 6.0, ((0, 256),))
    w_self = noise(key_of[1], (F, F), F ** -0.5, 0.25)
    w_neigh = noise(key_of[2], (F, F), F ** -0.5, 0.25)
    cotangent = noise(key_of[3], (TOTAL_V, F), 1.0, 6.0, ((0, 256),))
    neighbours = draw_neighbours(jax.random.fold_in(key_of[8], 71), 0)
    hub_slots = draw_hub_slots(jax.random.fold_in(key_of[8], 71), 0)
    send_rows = draw_send_rows(jax.random.fold_in(key_of[8], 71), 0)
    send_counts = draw_send_counts(jax.random.fold_in(key_of[8], 71), 0)
    return {"features": features, "w_self": w_self, "w_neigh": w_neigh, "cotangent": cotangent, "neighbours": neighbours, "hub_slots": hub_slots, "send_rows": send_rows, "send_counts": send_counts}


def sources(neighbours, hub_slots, send_rows, send_counts):
    total = V_DEV * N_DOM * N_SHARD
    rows = jnp.arange(total, dtype=jnp.int32)[:, None]
    device = rows // V_DEV
    group = device // N_SHARD
    place = device % N_SHARD
    slot = neighbours
    local_src = device * V_DEV + slot
    hub_index = jnp.clip(slot - V_DEV, 0, HUBS - 1)
    hub_src = (hub_index // HUB_DEV) * V_DEV + hub_slots[hub_index]
    bound = jnp.clip(slot - V_DEV - HUBS, 0, N_SHARD * CAP - 1)
    peer = bound // CAP
    within = bound % CAP
    sender = group * N_SHARD + peer
    live = within < send_counts[sender, place]
    bound_src = jnp.where(live, sender * V_DEV + send_rows[sender, place, within], total)
    src = jnp.where(slot < V_DEV, local_src, jnp.where(slot < V_DEV + HUBS, hub_src, jnp.where(slot < TABLE, bound_src, total)))
    return src.astype(jnp.int32)


def reference(features, w_self, w_neigh, cotangent, neighbours, hub_slots, send_rows, send_counts):
    total = V_DEV * N_DOM * N_SHARD
    width = features.shape[1]
    src = sources(neighbours, hub_slots, send_rows, send_counts)
    degree = jnp.sum(neighbours < TABLE, axis=1).astype(jnp.float32)
    padded = jnp.concatenate([features, jnp.zeros((1, width), jnp.bfloat16)], axis=0)
    blocks = src.reshape(total // V_DEV, V_DEV, DEG)
    sums = lax.map(lambda blk: jnp.sum(padded[blk], axis=1, dtype=jnp.float32), blocks).reshape(total, width)
    agg = (sums / degree[:, None]).astype(jnp.bfloat16)
    z = jnp.dot(features, w_self, preferred_element_type=jnp.float32) + jnp.dot(agg, w_neigh, preferred_element_type=jnp.float32)
    sig = jax.nn.sigmoid(z)
    hidden = (z * sig).astype(jnp.bfloat16)
    dz = (cotangent.astype(jnp.float32) * sig * (1.0 + z * (1.0 - sig))).astype(jnp.bfloat16)
    grad_self = jnp.dot(features.T, dz, preferred_element_type=jnp.float32)
    grad_neigh = jnp.dot(agg.T, dz, preferred_element_type=jnp.float32)
    edge_grad = jnp.dot(dz, w_neigh.T, preferred_element_type=jnp.float32) / degree[:, None]
    grads = edge_grad.reshape(total // V_DEV, V_DEV, width)

    def add_block(acc, pair):
        blk, grad = pair
        spread = jnp.broadcast_to(grad[:, None, :], (V_DEV, DEG, width)).reshape(-1, width)
        return acc.at[blk.reshape(-1)].add(spread), None

    start = jnp.zeros((total + 1, width), jnp.float32)
    accum, _ = lax.scan(add_block, start, (blocks, grads))
    grad_features = jnp.dot(dz, w_self.T, preferred_element_type=jnp.float32) + accum[:total]
    return hidden, grad_features, grad_self, grad_neigh
```

```python
import functools

import jax
import jax.numpy as jnp
from jax import lax
from jax.experimental import pallas as pl
from jax.experimental.pallas import tpu as pltpu
from jax.sharding import PartitionSpec as P

BF = jnp.bfloat16
F32 = jnp.float32
I32 = jnp.int32
PACK = 8
HUB_ROW = 4


def dot(a, b, ca=1, cb=0):
    return lax.dot_general(a, b, (((ca,), (cb,)), ((), ())), preferred_element_type=F32)


def call(kernel, outs, name, flops=0, nbytes=0, vmem=None):
    outs = [jax.ShapeDtypeStruct(s, d) for s, d in outs]
    spec = pl.BlockSpec(memory_space=pltpu.VMEM)

    def run(*args):
        return pl.pallas_call(
            kernel,
            out_shape=outs,
            in_specs=[spec] * len(args),
            out_specs=[spec] * len(outs),
            name=name,
            compiler_params=pltpu.CompilerParams(vmem_limit_bytes=vmem or (32 << 20)),
            cost_estimate=pl.CostEstimate(
                flops=flops or 1 << 20, bytes_accessed=nbytes or 1 << 20, transcendentals=0
            ),
        )(*args)

    return run


def place():
    dom = lax.axis_index("dom")
    return dom // 2, dom % 2


def iota(shape, dim):
    return lax.broadcasted_iota(I32, shape, dim)


def count_kernel(nb_ref, feat_ref, ws_ref, ct_ref, c_ref, deg_ref, zs_ref, s1_ref, *, table):
    verts, slots = nb_ref.shape
    packed = ct_ref.shape[0] - verts - 256
    y, c = place()
    nb = nb_ref[...]
    deg_ref[...] = jnp.sum((nb < table).astype(F32), axis=1, keepdims=True)
    nbt = nb.astype(F32).T.astype(I32)
    step = 64
    for t in range(0, ct_ref.shape[0], step):
        r = iota((step, verts), 0) + t
        if t < verts:
            want = r
        elif t < verts + packed:
            b = r - verts
            k = lax.rem(b, PACK)
            want = jnp.where(k < 4, verts + 256 + (b // PACK) * 4 + k, -1)
        else:
            block = (t - verts - packed) // 64
            i = r - (verts + packed + block * 64)
            dom = lax.rem(y - block + 4, 4) * 2
            want = verts + jnp.where(i < 32, (dom + c) * 32 + i, (dom + 1 - c) * 32 + i - 32)
        acc = jnp.zeros((step, verts), F32)
        for j in range(slots):
            acc = acc + jnp.where(nbt[j : j + 1, :] == want, 1.0, 0.0)
        ct_ref[t : t + step, :] = acc.astype(BF)
        c_ref[:, t : t + step] = acc.T.astype(BF)
    feat = feat_ref[...]
    zs_ref[...] = dot(feat, ws_ref[...])
    s1_ref[...] = dot(c_ref[:, :verts], feat)


def forward_kernel(
    feat_ref, cot_ref, wn_ref, c_ref, deg_ref, zs_ref, s1_ref, bnd_ref, h0_ref, hp_ref, h1_ref, h2_ref, h3_ref,
    hid_ref, dz_ref, send_ref, keep_ref,
):
    verts, width = feat_ref.shape
    _, c = place()
    packed = bnd_ref.shape[0] * PACK
    bnd = bnd_ref[...].reshape(packed, width)
    hubs = jnp.concatenate([h0_ref[...], hp_ref[...], h1_ref[...], h2_ref[...], h3_ref[...]], axis=0)
    sums = s1_ref[...] + dot(c_ref[:, verts : verts + packed], bnd) + dot(c_ref[:, verts + packed :], hubs)
    agg = (sums / deg_ref[...]).astype(BF)
    z = zs_ref[...] + dot(agg, wn_ref[...])
    sig = jax.nn.sigmoid(z)
    hid_ref[...] = (z * sig).astype(BF)
    dz = (cot_ref[...].astype(F32) * sig * (1.0 + z * (1.0 - sig))).astype(BF)
    dz_ref[...] = dz
    feat = feat_ref[...]
    first = c == 0
    send_ref[...] = dot(jnp.where(first, agg, feat), dz, 0, 0).astype(BF)
    keep_ref[...] = dot(jnp.where(first, feat, agg), dz, 0, 0)


def backward_kernel(dz_ref, wn_ref, ws_ref, deg_ref, ct_ref, base_ref, bnd_ref, hsend_ref, hkeep_ref):
    verts, width = dz_ref.shape
    packed = bnd_ref.shape[0]
    dz = dz_ref[...]
    edge = (dot(dz, wn_ref[...], 1, 1) / deg_ref[...]).astype(BF)
    base_ref[...] = dot(dz, ws_ref[...], 1, 1) + dot(ct_ref[:verts, :], edge)
    bnd_ref[...] = dot(ct_ref[verts : verts + packed, :], edge).astype(BF)
    hub = dot(ct_ref[verts + packed :, :], edge)
    for k in range(4):
        hkeep_ref[k] = hub[k * 64 : k * 64 + 32]
        hsend_ref[k] = hub[k * 64 + 32 : k * 64 + 64].astype(BF)


def half_kernel(keep_ref, got_ref, own_ref, s1_ref, s2_ref, s3_ref):
    y, _ = place()
    own_ref[...] = keep_ref[y] + got_ref[y].astype(F32)
    for k, ref in ((1, s1_ref), (2, s2_ref), (3, s3_ref)):
        j = lax.rem(y + k, 4)
        ref[...] = (keep_ref[j] + got_ref[j].astype(F32)).astype(BF)


def hub_half_kernel(keep_ref, got_ref, own_ref, s1_ref, s2_ref, s3_ref):
    own_ref[...] = keep_ref[0] + got_ref[0].astype(F32)
    for k, ref in ((1, s1_ref), (2, s2_ref), (3, s3_ref)):
        ref[...] = (keep_ref[k] + got_ref[k].astype(F32)).astype(BF)


def spread(rows, packed, first, per):
    r = iota((packed, rows), 0)
    k = lax.rem(r, PACK) - first
    pick = jnp.where((k >= 0) & (k < per), (r // PACK) * per + k, -1)
    return (pick == iota((packed, rows), 1)).astype(BF)


def second_pack_kernel(own_ref, r1_ref, r2_ref, r3_ref, bnd_ref, out_ref):
    w = own_ref[...] + r1_ref[...].astype(F32) + r2_ref[...].astype(F32) + r3_ref[...].astype(F32)
    packed, width = bnd_ref.shape
    out = bnd_ref[...].astype(F32) + dot(spread(w.shape[0], packed, 4, 4), w.astype(BF))
    out_ref[...] = out.astype(BF).reshape(out_ref.shape)


def third_pack_kernel(got_ref, own_ref, r1_ref, r2_ref, r3_ref, out_ref):
    peers, pack, width = got_ref.shape
    packed = peers * pack
    hub = own_ref[...] + r1_ref[...].astype(F32) + r2_ref[...].astype(F32) + r3_ref[...].astype(F32)
    rows = dot(spread(hub.shape[0], packed, HUB_ROW, 1), hub.astype(BF)).astype(BF)
    total = jnp.sum(got_ref[...].astype(F32), axis=0)
    low = jnp.concatenate([total[4:], jnp.zeros((4, width), F32)], axis=0)
    out_ref[...] = (rows.astype(F32).reshape(peers, pack, width) + low[None]).astype(BF)


def unpack_kernel(got_ref, out_ref):
    peers, pack, width = got_ref.shape
    packed = peers * pack
    rows = out_ref.shape[0]
    r = iota((rows, packed), 0)
    pick = (r // 4) * PACK + lax.rem(r, 4)
    sel = (pick == iota((rows, packed), 1)).astype(BF)
    out_ref[...] = dot(sel, got_ref[...].reshape(packed, width)).astype(BF)


def grad_kernel(base_ref, sel_ref, second_ref, third_ref, out_ref):
    peers, pack, width = second_ref.shape
    packed = peers * pack
    k = lax.rem(iota((packed, width), 0), PACK)
    second = second_ref[...].reshape(packed, width)
    third = third_ref[...].reshape(packed, width)
    zero = jnp.zeros_like(second)
    both = jnp.where(k < 4, second, jnp.where(k == HUB_ROW, third, zero))
    out_ref[...] = base_ref[...] + dot(sel_ref[...], both, 0, 0)


def weight_kernel(a0, a1, a2, a3, b0, b1, b2, b3, self_ref, neigh_ref):
    y, c = place()
    first = c == 0
    for k, (a, b) in enumerate(((a0, b0), (a1, b1), (a2, b2), (a3, b3))):
        j = lax.rem(y - k + 4, 4)
        mine, other = a[...].astype(F32), b[...].astype(F32)
        self_ref[j] = jnp.where(first, mine, other)
        neigh_ref[j] = jnp.where(first, other, mine)


def swap_core(x):
    return lax.ppermute(x, "dom", [(i, i ^ 1) for i in range(8)])


def shift_y(x, k):
    return lax.ppermute(x, "dom", [(i, ((i // 2 + k) % 4) * 2 + i % 2) for i in range(8)])


def exchange(x):
    return lax.all_to_all(x, "shard", split_axis=0, concat_axis=0, tiled=True)


def body(features, w_self, w_neigh, cotangent, neighbours, hub_slots, send_rows, send_counts):
    verts, width = features.shape
    peers, cap = send_rows.shape[1:]
    hubs = 256
    packed = peers * PACK
    table = verts + hubs + peers * cap
    rows = verts + packed + hubs

    slot = jnp.arange(PACK)[None, :]
    routes = jnp.pad(send_rows[0], ((0, 0), (0, PACK - cap)), constant_values=-1)
    index = jnp.where(slot < send_counts[0][:, None], routes, -1)
    index = jnp.where(slot == HUB_ROW, hub_slots[0], index)
    sel = (index[:, :, None] == jnp.arange(verts)).astype(BF).reshape(packed, verts)
    outgoing = dot(sel, features).astype(BF).reshape(peers, PACK, width)
    first = exchange(outgoing)

    ct, cm, degree, z_self, s_local = call(
        functools.partial(count_kernel, table=table),
        [((rows, verts), BF), ((verts, rows), BF), ((verts, 1), F32), ((verts, width), F32), ((verts, width), F32)],
        "count",
    )(neighbours, features, w_self)

    hub_own = first[:, HUB_ROW]
    hub_other = swap_core(hub_own)
    hub_pair = jnp.concatenate([hub_own, hub_other], axis=0)
    hub_far = [shift_y(hub_pair, k) for k in (1, 2, 3)]

    hidden, dz, w_send, w_keep = call(
        forward_kernel,
        [((verts, width), BF), ((verts, width), BF), ((width, width), BF), ((width, width), F32)],
        "forward",
    )(features, cotangent, w_neigh, cm, degree, z_self, s_local, first, hub_own, hub_other, *hub_far)

    w_got = swap_core(w_send)
    base, bnd_back, hub_send, hub_keep = call(
        backward_kernel,
        [((verts, width), F32), ((packed, width), BF), ((4, 32, width), BF), ((4, 32, width), F32)],
        "backward",
    )(dz, w_neigh, w_self, degree, ct)

    chunk = width // 4
    w_own, *w_out = call(half_kernel, [((chunk, width), F32)] + [((chunk, width), BF)] * 3, "half")(
        w_keep.reshape(4, chunk, width), w_got.reshape(4, chunk, width)
    )
    w_in = [shift_y(w_out[k - 1], k) for k in (1, 2, 3)]

    hub_got = swap_core(hub_send)
    h_own, *h_out = call(hub_half_kernel, [((32, width), F32)] + [((32, width), BF)] * 3, "hubhalf")(
        hub_keep, hub_got
    )
    h_in = [shift_y(h_out[k - 1], -k) for k in (1, 2, 3)]

    pack = call(second_pack_kernel, [((peers, PACK, width), BF)], "pack")(w_own, *w_in, bnd_back)[0]
    second = exchange(pack)
    pack = call(third_pack_kernel, [((peers, PACK, width), BF)], "pack2")(second, h_own, *h_in)[0]
    third = exchange(pack)
    w_part = call(unpack_kernel, [((chunk, width), BF)], "unpack")(third)[0]

    mine = [w_part] + [shift_y(w_part, k) for k in (1, 2, 3)]
    other = [swap_core(x) for x in mine]
    grad_features = call(grad_kernel, [((verts, width), F32)], "grad")(base, sel, second, third)[0]
    grad_self, grad_neigh = call(weight_kernel, [((4, chunk, width), F32)] * 2, "weights")(*mine, *other)
    return (hidden, grad_features, grad_self.reshape(width, width), grad_neigh.reshape(width, width))


def solution(mesh):
    vertex = P(("dom", "shard"), None)
    return jax.shard_map(
        body,
        mesh=mesh,
        in_specs=(
            vertex,
            P(),
            P(),
            vertex,
            vertex,
            P(("dom", "shard")),
            P(("dom", "shard"), None, None),
            vertex,
        ),
        out_specs=(vertex, vertex, P(), P()),
        check_vma=False,
    )
```

```python
import functools

import jax
import jax.numpy as jnp
from jax import lax
from jax.experimental import pallas as pl
from jax.experimental.pallas import tpu as pltpu
from jax.sharding import Mesh
from jax.sharding import PartitionSpec as P

BF = jnp.bfloat16
F32 = jnp.float32
I32 = jnp.int32
PACK = 8
HUB_ROW = 4
NY, NX, NZ = 4, 4, 8


def dot(a, b, ca=1, cb=0):
    return lax.dot_general(a, b, (((ca,), (cb,)), ((), ())), preferred_element_type=F32)


def call(kernel, outs, name, flops=1 << 22, nbytes=1 << 20, smem=()):
    outs = [jax.ShapeDtypeStruct(s, d) for s, d in outs]
    spec = pl.BlockSpec(memory_space=pltpu.VMEM)
    scalar = pl.BlockSpec(memory_space=pltpu.SMEM)

    def run(*args):
        return pl.pallas_call(
            kernel,
            out_shape=outs,
            in_specs=[scalar if i in smem else spec for i in range(len(args))],
            out_specs=[spec] * len(outs),
            name=name,
            compiler_params=pltpu.CompilerParams(vmem_limit_bytes=32 << 20),
            cost_estimate=pl.CostEstimate(flops=flops, bytes_accessed=nbytes, transcendentals=0),
        )(*args)

    return run


def place():
    dom = lax.axis_index("dom")
    return dom // 2, dom % 2


def iota(shape, dim):
    return lax.broadcasted_iota(I32, shape, dim)


def outgoing_kernel(slot_ref, feat_ref, route_ref, count_ref, out_ref, sel_ref):
    verts, width = feat_ref.shape
    cap, peers = route_ref.shape
    packed = peers * PACK
    live = iota((cap, peers), 0) < count_ref[...]
    routes = jnp.where(live, route_ref[...], -1).astype(F32).astype(BF)
    owner = (iota((packed, peers), 0) // PACK == iota((packed, peers), 1)).astype(BF)
    every = dot(owner, routes, 1, 1)
    k = lax.rem(iota((packed, cap), 0), PACK)
    index = jnp.sum(jnp.where(k == iota((packed, cap), 1), every, 0.0), axis=1, keepdims=True).astype(I32)
    k = lax.rem(iota((packed, 1), 0), PACK)
    index = jnp.where(k < cap, index, jnp.where(k == HUB_ROW, slot_ref[0], -1))
    sel = (index == iota((packed, verts), 1)).astype(BF)
    sel_ref[...] = sel
    out_ref[...] = dot(sel, feat_ref[...]).astype(BF).reshape(out_ref.shape)


def count_kernel(nbt_ref, feat_ref, ws_ref, sel_ref, ct_ref, c_ref, deg_ref, zs_ref, s1_ref, selt_ref, *, hubs, table):
    slots, verts = nbt_ref.shape
    packed = ct_ref.shape[0] // 2 - verts // 2
    far = verts + 2 * packed
    y, c = place()
    nbt = nbt_ref[...]
    degree = jnp.sum((nbt < table).astype(F32), axis=0, keepdims=True)
    deg_ref[...] = jnp.broadcast_to(degree, (8, verts)).T[:, :1]
    step = 128

    def hub(back, core, row):
        return verts + (lax.rem(y - back + NY, NY) * 2 + core) * NX * NZ + row

    for t in range(0, far + 256, step):
        r = iota((step, verts), 0)
        if t < verts:
            want = r + t
        elif t < far:
            mine = t < verts + packed
            b = r + (t - verts if mine else t - verts - packed)
            p, k = b // PACK, lax.rem(b, PACK)
            bound = verts + hubs + p * 4 + k if mine else -1
            want = jnp.where(k < 4, bound, hub(k - 4, c if mine else 1 - c, p))
        else:
            b = r + (t - far)
            i = b - 32
            p = lax.rem(i, 32)
            core = jnp.where(lax.rem(i // 32, 2) == 0, c, 1 - c)
            want = jnp.where(b < 32, hub(0, 1 - c, b), hub(i // 64 + 1, core, p))
            want = jnp.where(b < 224, want, -1)
        acc = jnp.zeros((step, verts), F32)
        for j in range(slots):
            acc = acc + jnp.where(nbt[j : j + 1, :] == want, 1.0, 0.0)
        if t < far:
            ct_ref[t : t + step, :] = acc.astype(BF)
        if t < verts + packed:
            c_ref[:, t : t + step] = acc.T.astype(BF)
        elif t >= far:
            t0 = t - packed
            c_ref[:, t0 : t0 + step] = acc.T.astype(BF)
    feat = feat_ref[...]
    zs_ref[...] = dot(feat, ws_ref[...])
    s1_ref[...] = dot(c_ref[:, :verts], feat)
    selt_ref[...] = sel_ref[...].astype(F32).T.astype(BF)


def forward_kernel(
    feat_ref, cot_ref, wn_ref, c_ref, deg_ref, zs_ref, s1_ref, bnd_ref, hp_ref, h1_ref, h2_ref, h3_ref,
    hid_ref, dz_ref, send_ref, keep_ref,
):
    verts, width = feat_ref.shape
    _, c = place()
    packed = bnd_ref.shape[0] * PACK
    bnd = bnd_ref[...].reshape(packed, width)
    pad = jnp.zeros((32, width), BF)
    hubs = jnp.concatenate([hp_ref[...], h1_ref[...], h2_ref[...], h3_ref[...], pad], axis=0)
    sums = s1_ref[...] + dot(c_ref[:, verts : verts + packed], bnd) + dot(c_ref[:, verts + packed :], hubs)
    agg = (sums / deg_ref[...]).astype(BF)
    z = zs_ref[...] + dot(agg, wn_ref[...])
    sig = jax.nn.sigmoid(z)
    hid_ref[...] = (z * sig).astype(BF)
    dz = (cot_ref[...].astype(F32) * sig * (1.0 + z * (1.0 - sig))).astype(BF)
    dz_ref[...] = dz
    feat = feat_ref[...]
    first = c == 0
    send_ref[...] = dot(jnp.where(first, agg, feat), dz, 0, 0).astype(BF)
    keep_ref[...] = dot(jnp.where(first, feat, agg), dz, 0, 0)


def backward_kernel(dz_ref, wn_ref, ws_ref, deg_ref, ct_ref, base_ref, mine_ref, other_ref):
    verts, width = dz_ref.shape
    packed = mine_ref.shape[0]
    dz = dz_ref[...]
    edge = (dot(dz, wn_ref[...], 1, 1) / deg_ref[...]).astype(BF)
    other_ref[...] = dot(ct_ref[verts + packed :, :], edge).astype(BF)
    mine_ref[...] = dot(ct_ref[verts : verts + packed, :], edge)
    base_ref[...] = dot(dz, ws_ref[...], 1, 1) + dot(ct_ref[:verts, :], edge)


def pair_kernel(mine_ref, got_ref, out_ref):
    out_ref[...] = (mine_ref[...] + got_ref[...].astype(F32)).astype(BF).reshape(out_ref.shape)


def half_kernel(keep_ref, got_ref, own_ref, s1_ref, s2_ref, s3_ref):
    y, _ = place()
    own_ref[...] = keep_ref[y] + got_ref[y].astype(F32)
    for k, ref in ((1, s1_ref), (2, s2_ref), (3, s3_ref)):
        j = lax.rem(y + k, NY)
        ref[...] = (keep_ref[j] + got_ref[j].astype(F32)).astype(BF)


def quarter_kernel(own_ref, r1_ref, r2_ref, r3_ref, out_ref, s1_ref, s2_ref, s3_ref):
    x = lax.axis_index("x")

    def chunk(j):
        return own_ref[j] + r1_ref[j].astype(F32) + r2_ref[j].astype(F32) + r3_ref[j].astype(F32)

    out_ref[...] = chunk(x)
    for k, ref in ((1, s1_ref), (2, s2_ref), (3, s3_ref)):
        ref[...] = chunk(lax.rem(x + k, NX)).astype(BF)


def column_kernel(own_ref, r1_ref, r2_ref, r3_ref, out_ref):
    total = own_ref[...] + r1_ref[...].astype(F32) + r2_ref[...].astype(F32) + r3_ref[...].astype(F32)
    out_ref[...] = jnp.broadcast_to(total.astype(BF)[None], out_ref.shape)


def total_kernel(got_ref, out_ref):
    out_ref[...] = jnp.sum(got_ref[...].astype(F32), axis=0).astype(BF)


def join_kernel(a0, a1, a2, a3, out_ref):
    x = lax.axis_index("x")
    for k, a in enumerate((a0, a1, a2, a3)):
        out_ref[lax.rem(x - k + NX, NX)] = a[...]


def hub_kernel(got_ref, out_ref):
    out_ref[...] = jnp.sum(got_ref[...].astype(F32), axis=0).astype(BF)


def grad_kernel(slot_ref, base_ref, selt_ref, got_ref, r1_ref, r2_ref, r3_ref, out_ref):
    verts, width = base_ref.shape
    got = got_ref[...].reshape(-1, width)
    far = sum(r[...].astype(F32)[HUB_ROW + k : HUB_ROW + k + 1] for k, r in ((1, r1_ref), (2, r2_ref), (3, r3_ref)))
    at = iota((verts, width), 0) == slot_ref[0]
    out_ref[...] = base_ref[...] + dot(selt_ref[...], got) + jnp.where(at, far, 0.0)


def weight_kernel(a0, a1, a2, a3, b0, b1, b2, b3, self_ref, neigh_ref):
    y, c = place()
    first = c == 0
    for k, (a, b) in enumerate(((a0, b0), (a1, b1), (a2, b2), (a3, b3))):
        j = lax.rem(y - k + NY, NY)
        mine, other = a[...].astype(F32), b[...].astype(F32)
        self_ref[j] = jnp.where(first, mine, other)
        neigh_ref[j] = jnp.where(first, other, mine)


def swap_core(v):
    return lax.ppermute(v, "dom", [(i, i ^ 1) for i in range(2 * NY)])


def shift_y(v, k):
    return lax.ppermute(v, "dom", [(i, ((i // 2 + k) % NY) * 2 + i % 2) for i in range(2 * NY)])


def shift_x(v, k):
    return lax.ppermute(v, "x", [(i, (i + k) % NX) for i in range(NX)])


def exchange(v, axis):
    return lax.all_to_all(v, axis, split_axis=0, concat_axis=0, tiled=True)


def body(features, w_self, w_neigh, cotangent, neighbours, hub_slots, send_rows, send_counts):
    verts, width = features.shape
    peers, cap = send_rows.shape[1:]
    hubs = 2 * NY * NX * NZ
    packed = peers * PACK
    table = verts + hubs + peers * cap

    outgoing, sel = call(
        outgoing_kernel, [((peers, PACK, width), BF), ((packed, verts), BF)], "outgoing", smem=(0,)
    )(hub_slots, features, send_rows[0].T, send_counts)
    first = exchange(outgoing, ("x", "z"))

    ct, cm, degree, z_self, s_local, selt = call(
        functools.partial(count_kernel, hubs=hubs, table=table),
        [
            ((verts + 2 * packed, verts), BF),
            ((verts, verts + packed + 256), BF),
            ((verts, 1), F32),
            ((verts, width), F32),
            ((verts, width), F32),
            ((verts, packed), BF),
        ],
        "count",
        flops=1 << 28,
        nbytes=1 << 23,
    )(neighbours.T, features, w_self, sel)

    first, ct, cm = lax.optimization_barrier((first, ct, cm))
    hub_own = first[:, HUB_ROW]
    hub_other = swap_core(hub_own)
    hub_pair = jnp.concatenate([hub_own, hub_other], axis=0)
    hub_far = [shift_y(hub_pair, k) for k in (1, 2, 3)]

    hidden, dz, w_send, w_keep = call(
        forward_kernel,
        [((verts, width), BF), ((verts, width), BF), ((width, width), BF), ((width, width), F32)],
        "forward",
    )(features, cotangent, w_neigh, cm, degree, z_self, s_local, first, hub_other, *hub_far)

    w_got = swap_core(w_send)
    base, mine, other = call(
        backward_kernel,
        [((verts, width), F32), ((packed, width), F32), ((packed, width), BF)],
        "backward",
    )(dz, w_neigh, w_self, degree, ct)
    other_got = swap_core(other)

    chunk = width // NY
    part = chunk // NX
    w_own, *w_out = call(half_kernel, [((chunk, width), F32)] + [((chunk, width), BF)] * 3, "half")(
        w_keep.reshape(NY, chunk, width), w_got.reshape(NY, chunk, width)
    )
    w_in = [shift_y(w_out[k - 1], k) for k in (1, 2, 3)]

    back = call(pair_kernel, [((peers, PACK, width), BF)], "pair")(mine, other_got)[0]
    second = exchange(back, ("x", "z"))

    split = (NX, part, width)
    w_own, *w_out = call(quarter_kernel, [((part, width), F32)] + [((part, width), BF)] * 3, "quarter")(
        w_own.reshape(split), *[w.reshape(split) for w in w_in]
    )
    w_in = [shift_x(w_out[k - 1], k) for k in (1, 2, 3)]
    w_col = call(column_kernel, [((NZ, part, width), BF)], "column")(w_own, *w_in)[0]
    w_sum = call(total_kernel, [((part, width), BF)], "total")(exchange(w_col, "z"))[0]

    hub_sum = call(hub_kernel, [((PACK, width), BF)], "hub")(second)[0]
    hub_in = [shift_y(hub_sum, -k) for k in (1, 2, 3)]
    grad_features = call(grad_kernel, [((verts, width), F32)], "grad", smem=(0,))(
        hub_slots, base, selt, second, *hub_in
    )[0]

    w_x = [w_sum] + [shift_x(w_sum, k) for k in (1, 2, 3)]
    w_part = call(join_kernel, [((NX, part, width), BF)], "join")(*w_x)[0].reshape(chunk, width)
    mine = [w_part] + [shift_y(w_part, k) for k in (1, 2, 3)]
    other = [swap_core(v) for v in mine]
    grad_self, grad_neigh = call(weight_kernel, [((NY, chunk, width), F32)] * 2, "weights")(*mine, *other)
    return (hidden, grad_features, grad_self.reshape(width, width), grad_neigh.reshape(width, width))


def solution(mesh):
    fine = Mesh(mesh.devices.reshape(2 * NY, NX, NZ), ("dom", "x", "z"))
    every = ("dom", "x", "z")
    vertex = P(every, None)
    return jax.shard_map(
        body,
        mesh=fine,
        in_specs=(vertex, P(), P(), vertex, vertex, P(every), P(every, None, None), vertex),
        out_specs=(vertex, vertex, P(), P()),
        check_vma=False,
    )
```

```python
import functools

import jax
import jax.numpy as jnp
from jax import lax
from jax.experimental import pallas as pl
from jax.experimental.pallas import tpu as pltpu
from jax.sharding import PartitionSpec as P

BF = jnp.bfloat16
F32 = jnp.float32
I32 = jnp.int32
PACK = 8
HUB = 4
NY = 4


def dot(a, b, ca=1, cb=0):
    return lax.dot_general(a, b, (((ca,), (cb,)), ((), ())), preferred_element_type=F32)


def call(kernel, outs, name, flops=1 << 22, nbytes=1 << 20, smem=(), hbm=(), hbm_out=False, scratch=(), alias=None):
    outs = [jax.ShapeDtypeStruct(s, d) for s, d in outs]
    vector = pl.BlockSpec(memory_space=pltpu.VMEM)
    scalar = pl.BlockSpec(memory_space=pltpu.SMEM)
    main = pl.BlockSpec(memory_space=pltpu.HBM)

    def run(*args):
        return pl.pallas_call(
            kernel,
            out_shape=outs,
            in_specs=[scalar if i in smem else main if i in hbm else vector for i in range(len(args))],
            out_specs=[main if hbm_out else vector] * len(outs),
            scratch_shapes=list(scratch),
            input_output_aliases=alias or {},
            name=name,
            compiler_params=pltpu.CompilerParams(vmem_limit_bytes=32 << 20),
            cost_estimate=pl.CostEstimate(flops=flops, bytes_accessed=nbytes, transcendentals=0),
        )(*args)

    return run


def place():
    dom = lax.axis_index("dom")
    return dom // 2, dom % 2


def iota(shape, dim):
    return lax.broadcasted_iota(I32, shape, dim)


def outgoing_kernel(sel_ref, feat_ref, r1_ref, r2_ref, r3_ref, out_ref):
    rows = dot(sel_ref[...], feat_ref[...])
    k = lax.rem(iota(rows.shape, 0), PACK)
    for i, ref in ((1, r1_ref), (2, r2_ref), (3, r3_ref)):
        rows = jnp.where(k == HUB + i, ref[...].astype(F32)[:1], rows)
    out_ref[...] = rows.astype(BF).reshape(out_ref.shape)


def packed_index(nb, verts, packed, hubs):
    y, c = place()
    h = nb - verts
    p, dom = lax.rem(h, 32), h // 32
    row = p * PACK + HUB + lax.rem(y - dom // 2 + NY, NY)
    hub = verts + row + jnp.where(lax.rem(dom, 2) == c, 0, packed)
    b = nb - verts - hubs
    bound = verts + (b // 4) * PACK + lax.rem(b, 4)
    far = jnp.where(nb < verts + hubs, hub, jnp.where(b < packed // 2, bound, -1))
    return jnp.where(nb < verts, nb, far)


def count_tile(index, at, step=128):
    slots, verts = index.shape
    rows = iota((step, verts), 0) + at
    acc = jnp.zeros((step, verts), F32)
    for j in range(slots):
        acc = acc + jnp.where(index[j : j + 1, :] == rows, 1.0, 0.0)
    return acc


def count_kernel(slot_ref, nbt_ref, route_ref, count_ref, ct_ref, c_ref, deg_ref, index_ref, sel_ref, *, hubs, table):
    packed, verts = sel_ref.shape
    cap, peers = route_ref.shape
    live = iota((cap, peers), 0) < count_ref[...]
    routes = jnp.where(live, route_ref[...], -1).astype(F32).astype(BF)
    owner = (iota((packed, peers), 0) // PACK == iota((packed, peers), 1)).astype(BF)
    every = dot(owner, routes, 1, 1)
    k = lax.rem(iota((packed, cap), 0), PACK)
    pick = jnp.sum(jnp.where(k == iota((packed, cap), 1), every, 0.0), axis=1, keepdims=True).astype(I32)
    k = lax.rem(iota((packed, 1), 0), PACK)
    pick = jnp.where(k < cap, pick, jnp.where(k == HUB, slot_ref[0], -1))
    sel_ref[...] = (pick == iota((packed, verts), 1)).astype(BF)

    nbt = nbt_ref[...]
    degree = jnp.sum((nbt < table).astype(F32), axis=0, keepdims=True)
    deg_ref[...] = jnp.broadcast_to(degree, (8, verts)).T[:, :1]
    index = packed_index(nbt, verts, packed, hubs)
    index_ref[...] = index
    for t in range(0, verts + packed, 128):
        acc = count_tile(index, t)
        ct_ref[t : t + 128, :] = acc.astype(BF)
        c_ref[:, t : t + 128] = acc.T.astype(BF)


def local_kernel(feat_ref, ws_ref, c_ref, index_ref, ct2_ref, c2_ref, zs_ref, s1_ref):
    feat = feat_ref[...]
    verts = feat.shape[0]
    zs_ref[...] = dot(feat, ws_ref[...])
    s1_ref[...] = dot(c_ref[:, :verts], feat)
    index = index_ref[...]
    for t in range(0, c2_ref.shape[1], 128):
        acc = count_tile(index, c_ref.shape[1] + t)
        ct2_ref[t : t + 128, :] = acc.astype(BF)
        c2_ref[:, t : t + 128] = acc.T.astype(BF)


def forward_kernel(
    feat_ref, cot_ref, wn_ref, c_ref, c2_ref, deg_ref, zs_ref, s1_ref, got_ref, other_ref,
    hid_ref, dz_ref, send_ref, keep_ref,
):
    verts, width = feat_ref.shape
    _, c = place()
    got = got_ref[...].reshape(-1, width)
    other = other_ref[...].reshape(-1, width)
    sums = s1_ref[...] + dot(c_ref[:, verts:], got) + dot(c2_ref[...], other)
    agg = (sums / deg_ref[...]).astype(BF)
    z = zs_ref[...] + dot(agg, wn_ref[...])
    sig = jax.nn.sigmoid(z)
    hid_ref[...] = (z * sig).astype(BF)
    dz = (cot_ref[...].astype(F32) * sig * (1.0 + z * (1.0 - sig))).astype(BF)
    dz_ref[...] = dz
    feat = feat_ref[...]
    first = c == 0
    send_ref[...] = dot(jnp.where(first, agg, feat), dz, 0, 0).astype(BF)
    keep_ref[...] = dot(jnp.where(first, feat, agg), dz, 0, 0)


def backward_kernel(dz_ref, wn_ref, ws_ref, deg_ref, ct_ref, ct2_ref, base_ref, mine_ref, other_ref):
    verts, width = dz_ref.shape
    dz = dz_ref[...]
    edge = (dot(dz, wn_ref[...], 1, 1) / deg_ref[...]).astype(BF)
    other_ref[...] = dot(ct2_ref[...], edge).astype(BF)
    mine_ref[...] = dot(ct_ref[verts:, :], edge)
    base_ref[...] = dot(dz, ws_ref[...], 1, 1) + dot(ct_ref[:verts, :], edge)


def half_kernel(keep_ref, got_ref, own_ref, s1_ref, s2_ref, s3_ref):
    y, _ = place()
    own_ref[...] = keep_ref[y] + got_ref[y].astype(F32)
    for k, ref in ((1, s1_ref), (2, s2_ref), (3, s3_ref)):
        j = lax.rem(y + k, 4)
        ref[...] = (keep_ref[j] + got_ref[j].astype(F32)).astype(BF)


def spread(rows, packed, first, per):
    r = iota((packed, rows), 0)
    k = lax.rem(r, PACK) - first
    pick = jnp.where((k >= 0) & (k < per), (r // PACK) * per + k, -1)
    return (pick == iota((packed, rows), 1)).astype(BF)


def second_pack_kernel(own_ref, r1_ref, r2_ref, r3_ref, mine_ref, out_ref):
    w = own_ref[...] + r1_ref[...].astype(F32) + r2_ref[...].astype(F32) + r3_ref[...].astype(F32)
    mine = mine_ref[...]
    packed = mine.shape[0]
    rows = dot(spread(w.shape[0], packed, HUB, 4), w.astype(BF))
    k = lax.rem(iota(mine.shape, 0), PACK)
    out_ref[...] = jnp.where(k < HUB, mine, rows).astype(BF).reshape(out_ref.shape)


def third_pack_kernel(got_ref, mine_ref, other_ref, out_ref):
    peers, pack, width = got_ref.shape
    hub = (mine_ref[...] + other_ref[...].astype(F32)).reshape(peers, pack, width)
    total = jnp.sum(got_ref[...].astype(F32), axis=0)
    total = jnp.concatenate([total[HUB:], total[HUB:]], axis=0)
    k = iota((peers, pack, width), 1)
    out_ref[...] = jnp.where(k < HUB, total[None], hub).astype(BF)


def unpack_kernel(got_ref, out_ref):
    peers, pack, width = got_ref.shape
    packed = peers * pack
    rows = out_ref.shape[0] - pack
    r = iota((rows, packed), 0)
    pick = (r // 4) * PACK + lax.rem(r, 4)
    sel = (pick == iota((rows, packed), 1)).astype(BF)
    got = got_ref[...]
    out_ref[:rows, :] = dot(sel, got.reshape(packed, width)).astype(BF)
    out_ref[rows:, :] = jnp.sum(got.astype(F32), axis=0).astype(BF)


def grad_kernel(slot_ref, base_ref, sel_ref, got_ref, own_ref, r1_ref, r2_ref, r3_ref, out_ref):
    verts, width = base_ref.shape
    got = got_ref[...].reshape(-1, width)
    k = lax.rem(iota(got.shape, 0), PACK)
    got = jnp.where(k < HUB, got, jnp.zeros_like(got))
    hub = jnp.zeros((1, width), F32)
    for i, ref in ((0, own_ref), (3, r1_ref), (2, r2_ref), (1, r3_ref)):
        tail = ref[ref.shape[0] - PACK :, :].astype(F32)
        hub = hub + tail[HUB + i : HUB + i + 1]
    at = iota((verts, width), 0) == slot_ref[0]
    out_ref[...] = base_ref[...] + dot(sel_ref[...], got, 0, 0) + jnp.where(at, hub, 0.0)


def weight_kernel(a0, a1, a2, a3, b0, b1, b2, b3, self_ref, neigh_ref):
    y, c = place()
    first = c == 0
    rows = self_ref.shape[1]
    for k, (a, b) in enumerate(((a0, b0), (a1, b1), (a2, b2), (a3, b3))):
        j = lax.rem(y - k + NY, NY)
        mine, other = a[:rows, :].astype(F32), b[:rows, :].astype(F32)
        self_ref[j] = jnp.where(first, mine, other)
        neigh_ref[j] = jnp.where(first, other, mine)


def swap_core(x):
    return lax.ppermute(x, "dom", [(i, i ^ 1) for i in range(8)])


def shift_y(x, k):
    return lax.ppermute(x, "dom", [(i, ((i // 2 + k) % 4) * 2 + i % 2) for i in range(8)])


def exchange(x):
    return lax.all_to_all(x, "shard", split_axis=0, concat_axis=0, tiled=True)


def body(features, w_self, w_neigh, cotangent, neighbours, hub_slots, send_rows, send_counts):
    verts, width = features.shape
    peers, cap = send_rows.shape[1:]
    hubs = 256
    packed = peers * PACK
    table = verts + hubs + peers * cap
    rows = verts + packed

    hub_row = lax.dynamic_slice(features, (hub_slots[0].astype(jnp.uint32), jnp.uint32(0)), (1, width))
    hub_in = [shift_y(hub_row, k) for k in (1, 2, 3)]
    ct, cm, degree, index, sel = call(
        functools.partial(count_kernel, hubs=hubs, table=table),
        [
            ((rows, verts), BF),
            ((verts, rows), BF),
            ((verts, 1), F32),
            (neighbours.shape[::-1], I32),
            ((packed, verts), BF),
        ],
        "count",
        flops=1 << 28,
        smem=(0,),
    )(hub_slots, neighbours.T, send_rows[0].T, send_counts)
    outgoing = call(outgoing_kernel, [((peers, PACK, width), BF)], "outgoing")(sel, features, *hub_in)[0]
    first = exchange(outgoing)
    first_other = swap_core(first)
    ct2, cm2, z_self, s_local = call(
        local_kernel,
        [((packed, verts), BF), ((verts, packed), BF), ((verts, width), F32), ((verts, width), F32)],
        "local",
    )(features, w_self, cm, index)

    hidden, dz, w_send, w_keep = call(
        forward_kernel,
        [((verts, width), BF), ((verts, width), BF), ((width, width), BF), ((width, width), F32)],
        "forward",
    )(features, cotangent, w_neigh, cm, cm2, degree, z_self, s_local, first, first_other)

    w_got = swap_core(w_send)
    base, mine, other = call(
        backward_kernel,
        [((verts, width), F32), ((packed, width), F32), ((packed, width), BF)],
        "backward",
    )(dz, w_neigh, w_self, degree, ct, ct2)

    chunk = width // NY
    w_own, *w_out = call(half_kernel, [((chunk, width), F32)] + [((chunk, width), BF)] * 3, "half")(
        w_keep.reshape(NY, chunk, width), w_got.reshape(NY, chunk, width)
    )
    w_in = [shift_y(w_out[k - 1], k) for k in (1, 2, 3)]

    mine, other = lax.optimization_barrier((mine, swap_core(other)))
    pack = call(second_pack_kernel, [((peers, PACK, width), BF)], "pack")(w_own, *w_in, mine)[0]
    second = exchange(pack)
    pack = call(third_pack_kernel, [((peers, PACK, width), BF)], "pack2")(second, mine, other)[0]
    third = exchange(pack)
    w_part = call(unpack_kernel, [((chunk + PACK, width), BF)], "unpack")(third)[0]

    w_all = [w_part] + [shift_y(w_part, k) for k in (1, 2, 3)]
    w_other = [swap_core(v) for v in w_all]
    grad_features = call(grad_kernel, [((verts, width), F32)], "grad", smem=(0,))(
        hub_slots, base, sel, second, *w_all
    )[0]
    grad_self, grad_neigh = call(weight_kernel, [((NY, chunk, width), F32)] * 2, "weights")(*w_all, *w_other)
    return (hidden, grad_features, grad_self.reshape(width, width), grad_neigh.reshape(width, width))


def solution(mesh):
    vertex = P(("dom", "shard"), None)
    return jax.shard_map(
        body,
        mesh=mesh,
        in_specs=(
            vertex,
            P(),
            P(),
            vertex,
            vertex,
            P(("dom", "shard")),
            P(("dom", "shard"), None, None),
            vertex,
        ),
        out_specs=(vertex, vertex, P(), P()),
        check_vma=False,
    )
```

```python
import functools

import jax
import jax.numpy as jnp
from jax import lax
from jax.experimental import pallas as pl
from jax.experimental.pallas import tpu as pltpu
from jax.sharding import Mesh
from jax.sharding import PartitionSpec as P

BF = jnp.bfloat16
F32 = jnp.float32
I32 = jnp.int32
PACK = 8
HUB = 4
NY, NX, NZ = 4, 4, 8


def dot(a, b, ca=1, cb=0):
    return lax.dot_general(a, b, (((ca,), (cb,)), ((), ())), preferred_element_type=F32)


def call(kernel, outs, name, flops=1 << 22, nbytes=1 << 20, smem=(), hbm=(), hbm_out=False, scratch=(), alias=None):
    outs = [jax.ShapeDtypeStruct(s, d) for s, d in outs]
    vector = pl.BlockSpec(memory_space=pltpu.VMEM)
    scalar = pl.BlockSpec(memory_space=pltpu.SMEM)
    main = pl.BlockSpec(memory_space=pltpu.HBM)

    def run(*args):
        return pl.pallas_call(
            kernel,
            out_shape=outs,
            in_specs=[scalar if i in smem else main if i in hbm else vector for i in range(len(args))],
            out_specs=[main if hbm_out else vector] * len(outs),
            scratch_shapes=list(scratch),
            input_output_aliases=alias or {},
            name=name,
            compiler_params=pltpu.CompilerParams(vmem_limit_bytes=32 << 20),
            cost_estimate=pl.CostEstimate(flops=flops, bytes_accessed=nbytes, transcendentals=0),
        )(*args)

    return run


def place():
    return lax.axis_index("y"), lax.axis_index("c")


def iota(shape, dim):
    return lax.broadcasted_iota(I32, shape, dim)


def outgoing_kernel(sel_ref, feat_ref, r1_ref, r2_ref, r3_ref, out_ref):
    rows = dot(sel_ref[...], feat_ref[...])
    k = lax.rem(iota(rows.shape, 0), PACK)
    for i, ref in ((1, r1_ref), (2, r2_ref), (3, r3_ref)):
        rows = jnp.where(k == HUB + i, ref[...].astype(F32)[:1], rows)
    out_ref[...] = rows.astype(BF).reshape(out_ref.shape)


def packed_index(nb, verts, packed, hubs):
    y, c = place()
    h = nb - verts
    p, dom = lax.rem(h, 32), h // 32
    row = p * PACK + HUB + lax.rem(y - dom // 2 + NY, NY)
    hub = verts + row + jnp.where(lax.rem(dom, 2) == c, 0, packed)
    b = nb - verts - hubs
    bound = verts + (b // 4) * PACK + lax.rem(b, 4)
    far = jnp.where(nb < verts + hubs, hub, jnp.where(b < packed // 2, bound, -1))
    return jnp.where(nb < verts, nb, far)


def count_tile(index, at, step=128):
    slots, verts = index.shape
    index = jnp.clip(index - at, -1, step).astype(F32).astype(BF)
    rows = iota((step, verts), 0).astype(F32).astype(BF)
    one, zero = jnp.ones((), BF), jnp.zeros((), BF)
    acc = jnp.zeros((step, verts), BF)
    for j in range(slots):
        acc = acc + jnp.where(index[j : j + 1, :] == rows, one, zero)
    return acc


def count_kernel(slot_ref, nbt_ref, route_ref, count_ref, ct_ref, c_ref, deg_ref, index_ref, sel_ref, *, hubs, table):
    packed, verts = sel_ref.shape
    cap, peers = route_ref.shape
    live = iota((cap, peers), 0) < count_ref[...]
    routes = jnp.where(live, route_ref[...], -1).astype(F32).astype(BF)
    owner = (iota((packed, peers), 0) // PACK == iota((packed, peers), 1)).astype(BF)
    every = dot(owner, routes, 1, 1)
    k = lax.rem(iota((packed, cap), 0), PACK)
    pick = jnp.sum(jnp.where(k == iota((packed, cap), 1), every, 0.0), axis=1, keepdims=True).astype(I32)
    k = lax.rem(iota((packed, 1), 0), PACK)
    pick = jnp.where(k < cap, pick, jnp.where(k == HUB, slot_ref[0], -1))
    sel_ref[...] = (pick == iota((packed, verts), 1)).astype(BF)

    nbt = nbt_ref[...]
    degree = jnp.sum((nbt < table).astype(F32), axis=0, keepdims=True)
    deg_ref[...] = jnp.broadcast_to(degree, (8, verts)).T[:, :1]
    index = packed_index(nbt, verts, packed, hubs)
    index_ref[...] = index
    for t in range(0, verts + packed, 128):
        acc = count_tile(index, t)
        ct_ref[t : t + 128, :] = acc
        c_ref[:, t : t + 128] = acc.astype(F32).T.astype(BF)


def local_kernel(feat_ref, ws_ref, c_ref, index_ref, ct2_ref, c2_ref, zs_ref, s1_ref):
    feat = feat_ref[...]
    verts = feat.shape[0]
    zs_ref[...] = dot(feat, ws_ref[...])
    s1_ref[...] = dot(c_ref[:, :verts], feat)
    index = index_ref[...]
    for t in range(0, c2_ref.shape[1], 128):
        acc = count_tile(index, c_ref.shape[1] + t)
        ct2_ref[t : t + 128, :] = acc
        c2_ref[:, t : t + 128] = acc.astype(F32).T.astype(BF)


def forward_kernel(
    feat_ref, cot_ref, wn_ref, c_ref, c2_ref, deg_ref, zs_ref, s1_ref, got_ref, other_ref,
    hid_ref, dz_ref, send_ref, keep_ref,
):
    verts, width = feat_ref.shape
    _, c = place()
    got = got_ref[...].reshape(-1, width)
    other = other_ref[...].reshape(-1, width)
    sums = s1_ref[...] + dot(c_ref[:, verts:], got) + dot(c2_ref[...], other)
    agg = (sums / deg_ref[...]).astype(BF)
    z = zs_ref[...] + dot(agg, wn_ref[...])
    sig = jax.nn.sigmoid(z)
    hid_ref[...] = (z * sig).astype(BF)
    dz = (cot_ref[...].astype(F32) * sig * (1.0 + z * (1.0 - sig))).astype(BF)
    dz_ref[...] = dz
    feat = feat_ref[...]
    first = c == 0
    send_ref[...] = dot(jnp.where(first, agg, feat), dz, 0, 0).astype(BF)
    keep_ref[...] = dot(jnp.where(first, feat, agg), dz, 0, 0)


def backward_kernel(dz_ref, wn_ref, ws_ref, deg_ref, ct_ref, ct2_ref, base_ref, mine_ref, other_ref):
    verts, width = dz_ref.shape
    dz = dz_ref[...]
    edge = (dot(dz, wn_ref[...], 1, 1) / deg_ref[...]).astype(BF)
    other_ref[...] = dot(ct2_ref[...], edge).astype(BF)
    mine_ref[...] = dot(ct_ref[verts:, :], edge)
    base_ref[...] = dot(dz, ws_ref[...], 1, 1) + dot(ct_ref[:verts, :], edge)


def half_kernel(keep_ref, got_ref, out_ref):
    out_ref[...] = (keep_ref[...] + got_ref[...].astype(F32)).astype(BF).reshape(out_ref.shape)


def pair_kernel(mine_ref, got_ref, own_ref, s1_ref, s2_ref, s3_ref):
    x = lax.axis_index("x")
    for k, ref in enumerate((own_ref, s1_ref, s2_ref, s3_ref)):
        j = lax.rem(x + k, NX)
        ref[...] = (mine_ref[j] + got_ref[j].astype(F32)).astype(BF)


def join(a, b):
    return jnp.concatenate([a[:, :HUB], b[:, :HUB]], axis=1)


def packs(ref):
    return ref[...].astype(F32).reshape(-1, PACK, ref.shape[-1])


def pack_kernel(got_ref, own_ref, r1_ref, r2_ref, r3_ref, out_ref):
    rows = got_ref.shape[1]
    total = jnp.sum(got_ref[...].astype(F32), axis=0).astype(BF)
    out_ref[:, :rows, :] = jnp.broadcast_to(total[None], (NZ,) + total.shape)
    own, r1, r2, r3 = (packs(r) for r in (own_ref, r1_ref, r2_ref, r3_ref))
    k = iota(own.shape, 1)
    first = jnp.where(k < HUB, own, own + r1 + r2 + r3)
    out_ref[:, rows : rows + PACK, :] = first.astype(BF)
    out_ref[:, rows + PACK : rows + 2 * PACK, :] = join(r1, r2).astype(BF)
    out_ref[:, rows + 2 * PACK :, :] = join(r3, jnp.zeros_like(r3)).astype(BF)


def unpack_kernel(got_ref, out_ref, hub_ref):
    rows = out_ref.shape[1]
    total = jnp.sum(got_ref[:, :rows, :].astype(F32), axis=0).astype(BF)
    out_ref[...] = jnp.broadcast_to(total[None], out_ref.shape)
    hub_ref[...] = jnp.sum(got_ref[:, rows : rows + PACK, :].astype(F32), axis=0).astype(BF)


def grad_kernel(slot_ref, base_ref, sel_ref, got_ref, r1_ref, r2_ref, r3_ref, out_ref):
    verts, width = base_ref.shape
    x = lax.axis_index("x")
    rows = got_ref.shape[1] - 3 * PACK
    block = NZ * PACK
    own = sel_ref[x]
    b1, b2, b3 = (sel_ref[lax.rem(x - k + NX, NX)].astype(F32).reshape(NZ, PACK, verts) for k in (1, 2, 3))
    pair = join(b1, b2).reshape(block, verts).astype(BF)
    last = join(b3, jnp.zeros_like(b3)).reshape(block, verts).astype(BF)
    out = base_ref[...]
    for i, sel in enumerate((own, pair, last)):
        at = rows + i * PACK
        out = out + dot(sel, got_ref[:, at : at + PACK, :].reshape(block, width), 0, 0)
    hub = jnp.zeros((1, width), F32)
    for i, ref in ((3, r1_ref), (2, r2_ref), (1, r3_ref)):
        hub = hub + ref[...].astype(F32)[HUB + i : HUB + i + 1]
    out_ref[...] = out + jnp.where(iota((verts, width), 0) == slot_ref[0], hub, 0.0)


def weight_kernel(mine_ref, other_ref, self_ref, neigh_ref):
    _, c = place()
    first = c == 0
    mine, other = mine_ref[...].astype(F32), other_ref[...].astype(F32)
    self_ref[...] = jnp.where(first, mine, other)
    neigh_ref[...] = jnp.where(first, other, mine)


def swap_core(v):
    return lax.ppermute(v, "c", [(0, 1), (1, 0)])


def shift(v, axis, k):
    return lax.ppermute(v, axis, [(i, (i + k) % 4) for i in range(4)])


def exchange(v, axes):
    return lax.all_to_all(v, axes, split_axis=0, concat_axis=0, tiled=True)


def body(features, w_self, w_neigh, cotangent, neighbours, hub_slots, send_rows, send_counts):
    verts, width = features.shape
    peers, cap = send_rows.shape[1:]
    hubs = 256
    packed = peers * PACK
    table = verts + hubs + peers * cap
    rows = verts + packed

    hub_row = lax.dynamic_slice(features, (hub_slots[0].astype(jnp.uint32), jnp.uint32(0)), (1, width))
    hub_in = [shift(hub_row, "y", k) for k in (1, 2, 3)]
    ct, cm, degree, index, sel = call(
        functools.partial(count_kernel, hubs=hubs, table=table),
        [
            ((rows, verts), BF),
            ((verts, rows), BF),
            ((verts, 1), F32),
            (neighbours.shape[::-1], I32),
            ((packed, verts), BF),
        ],
        "count",
        flops=1 << 28,
        smem=(0,),
    )(hub_slots, neighbours.T, send_rows[0].T, send_counts)
    outgoing = call(outgoing_kernel, [((peers, PACK, width), BF)], "outgoing")(sel, features, *hub_in)[0]
    first = exchange(outgoing, ("x", "z"))
    first_other = swap_core(first)
    ct2, cm2, z_self, s_local = call(
        local_kernel,
        [((packed, verts), BF), ((verts, packed), BF), ((verts, width), F32), ((verts, width), F32)],
        "local",
    )(features, w_self, cm, index)

    hidden, dz, w_send, w_keep = call(
        forward_kernel,
        [((verts, width), BF), ((verts, width), BF), ((width, width), BF), ((width, width), F32)],
        "forward",
    )(features, cotangent, w_neigh, cm, cm2, degree, z_self, s_local, first, first_other)

    w_got = swap_core(w_send)
    base, mine, other = call(
        backward_kernel,
        [((verts, width), F32), ((packed, width), F32), ((packed, width), BF)],
        "backward",
    )(dz, w_neigh, w_self, degree, ct, ct2)

    part = width // (NY * NX)
    other_got = swap_core(other)
    w_keep, mine = lax.optimization_barrier((w_keep, mine))
    blocks = call(half_kernel, [((NY * NX, part, width), BF)], "half")(w_keep, w_got)[0]
    second = exchange(blocks, ("y", "x"))

    split = (NX, NZ * PACK, width)
    b_own, *b_out = call(pair_kernel, [(split[1:], BF)] * 4, "pair")(
        mine.reshape(split), other_got.reshape(split)
    )
    b_in = [shift(b_out[k - 1], "x", k) for k in (1, 2, 3)]
    pack = call(pack_kernel, [((NZ, part + 3 * PACK, width), BF)], "pack")(second, b_own, *b_in)[0]
    third = exchange(pack, "z")
    copies, hub = call(unpack_kernel, [((NY * NX, part, width), BF), ((PACK, width), BF)], "unpack")(third)
    fourth = exchange(copies, ("y", "x")).reshape(width, width)
    hub_back = [shift(hub, "y", k) for k in (1, 2, 3)]
    fourth, hub_back = lax.optimization_barrier((fourth, hub_back))
    grad_features = call(grad_kernel, [((verts, width), F32)], "grad", smem=(0,))(
        hub_slots, base, sel.reshape(NX, NZ * PACK, verts), third, *hub_back
    )[0]
    grad_self, grad_neigh = call(weight_kernel, [((width, width), F32)] * 2, "weights")(fourth, swap_core(fourth))
    return (hidden, grad_features, grad_self, grad_neigh)


def solution(mesh):
    every = ("y", "c", "x", "z")
    fine = Mesh(mesh.devices.reshape(NY, 2, NX, NZ), every)
    vertex = P(every, None)
    return jax.shard_map(
        body,
        mesh=fine,
        in_specs=(vertex, P(), P(), vertex, vertex, P(every), P(every, None, None), vertex),
        out_specs=(vertex, vertex, P(), P()),
        check_vma=False,
    )
```

```python
import functools

import jax
import jax.numpy as jnp
from jax import lax
from jax.experimental import pallas as pl
from jax.experimental.pallas import tpu as pltpu
from jax.sharding import Mesh
from jax.sharding import PartitionSpec as P

BF = jnp.bfloat16
F32 = jnp.float32
I32 = jnp.int32
PACK = 8
HUB = 4
NY, NX, NZ = 4, 4, 8


def dot(a, b, ca=1, cb=0):
    return lax.dot_general(a, b, (((ca,), (cb,)), ((), ())), preferred_element_type=F32)


def call(kernel, outs, name, flops=1 << 22, nbytes=1 << 20, smem=(), hbm=(), hbm_out=False, scratch=(), alias=None):
    outs = [jax.ShapeDtypeStruct(s, d) for s, d in outs]
    vector = pl.BlockSpec(memory_space=pltpu.VMEM)
    scalar = pl.BlockSpec(memory_space=pltpu.SMEM)
    main = pl.BlockSpec(memory_space=pltpu.HBM)

    def run(*args):
        return pl.pallas_call(
            kernel,
            out_shape=outs,
            in_specs=[scalar if i in smem else main if i in hbm else vector for i in range(len(args))],
            out_specs=[main if hbm_out else vector] * len(outs),
            scratch_shapes=list(scratch),
            input_output_aliases=alias or {},
            name=name,
            compiler_params=pltpu.CompilerParams(vmem_limit_bytes=32 << 20),
            cost_estimate=pl.CostEstimate(flops=flops, bytes_accessed=nbytes, transcendentals=0),
        )(*args)

    return run


def place():
    return lax.axis_index("y"), lax.axis_index("c")


def iota(shape, dim):
    return lax.broadcasted_iota(I32, shape, dim)


def outgoing_kernel(slot_ref, route_ref, count_ref, feat_ref, r1_ref, r2_ref, r3_ref, out_ref, sel_ref):
    packed, verts = sel_ref.shape
    cap, peers = route_ref.shape
    live = iota((cap, peers), 0) < count_ref[...]
    routes = jnp.where(live, route_ref[...], -1).astype(F32).astype(BF)
    owner = (iota((packed, peers), 0) // PACK == iota((packed, peers), 1)).astype(BF)
    every = dot(owner, routes, 1, 1)
    k = lax.rem(iota((packed, cap), 0), PACK)
    pick = jnp.sum(jnp.where(k == iota((packed, cap), 1), every, 0.0), axis=1, keepdims=True).astype(I32)
    k = lax.rem(iota((packed, 1), 0), PACK)
    pick = jnp.where(k < cap, pick, jnp.where(k == HUB, slot_ref[0], -1))
    sel = (pick == iota((packed, verts), 1)).astype(BF)
    sel_ref[...] = sel
    rows = dot(sel, feat_ref[...])
    k = lax.rem(iota(rows.shape, 0), PACK)
    for i, ref in ((1, r1_ref), (2, r2_ref), (3, r3_ref)):
        rows = jnp.where(k == HUB + i, ref[...].astype(F32)[:1], rows)
    out_ref[...] = rows.astype(BF).reshape(out_ref.shape)


def packed_index(nb, verts, packed, hubs):
    y, c = place()
    h = nb - verts
    p, dom = lax.rem(h, 32), h // 32
    row = p * PACK + HUB + lax.rem(y - dom // 2 + NY, NY)
    hub = verts + row + jnp.where(lax.rem(dom, 2) == c, 0, packed)
    b = nb - verts - hubs
    bound = verts + (b // 4) * PACK + lax.rem(b, 4)
    far = jnp.where(nb < verts + hubs, hub, jnp.where(b < packed // 2, bound, -1))
    return jnp.where(nb < verts, nb, far)


def count_tile(index, at, step=128):
    slots, verts = index.shape
    index = jnp.clip(index - at, -1, step).astype(F32).astype(BF)
    rows = iota((step, verts), 0).astype(F32).astype(BF)
    one, zero = jnp.ones((), BF), jnp.zeros((), BF)
    acc = jnp.zeros((step, verts), BF)
    for j in range(slots):
        acc = acc + jnp.where(index[j : j + 1, :] == rows, one, zero)
    return acc


def count_kernel(nbt_ref, ct_ref, c_ref, deg_ref, index_ref, *, packed, hubs, table):
    verts = nbt_ref.shape[1]
    nbt = nbt_ref[...]
    degree = jnp.sum((nbt < table).astype(F32), axis=0, keepdims=True)
    deg_ref[...] = jnp.broadcast_to(degree, (8, verts)).T[:, :1]
    index = packed_index(nbt, verts, packed, hubs)
    index_ref[...] = index
    for t in range(0, verts + packed, 128):
        acc = count_tile(index, t)
        ct_ref[t : t + 128, :] = acc
        c_ref[:, t : t + 128] = acc.astype(F32).T.astype(BF)


def local_kernel(feat_ref, ws_ref, c_ref, index_ref, ct2_ref, c2_ref, zs_ref, s1_ref):
    feat = feat_ref[...]
    verts = feat.shape[0]
    zs_ref[...] = dot(feat, ws_ref[...])
    s1_ref[...] = dot(c_ref[:, :verts], feat)
    index = index_ref[...]
    for t in range(0, c2_ref.shape[1], 128):
        acc = count_tile(index, c_ref.shape[1] + t)
        ct2_ref[t : t + 128, :] = acc
        c2_ref[:, t : t + 128] = acc.astype(F32).T.astype(BF)


def forward_kernel(
    feat_ref, cot_ref, wn_ref, c_ref, c2_ref, deg_ref, zs_ref, s1_ref, got_ref, other_ref,
    hid_ref, dz_ref, send_ref, keep_ref,
):
    verts, width = feat_ref.shape
    _, c = place()
    got = got_ref[...].reshape(-1, width)
    other = other_ref[...].reshape(-1, width)
    sums = s1_ref[...] + dot(c_ref[:, verts:], got) + dot(c2_ref[...], other)
    agg = (sums / deg_ref[...]).astype(BF)
    z = zs_ref[...] + dot(agg, wn_ref[...])
    sig = jax.nn.sigmoid(z)
    hid_ref[...] = (z * sig).astype(BF)
    dz = (cot_ref[...].astype(F32) * sig * (1.0 + z * (1.0 - sig))).astype(BF)
    dz_ref[...] = dz
    feat = feat_ref[...]
    first = c == 0
    send_ref[...] = dot(jnp.where(first, agg, feat), dz, 0, 0).astype(BF)
    keep_ref[...] = dot(jnp.where(first, feat, agg), dz, 0, 0)


def backward_kernel(dz_ref, wn_ref, ws_ref, deg_ref, ct_ref, ct2_ref, base_ref, mine_ref, other_ref):
    verts, width = dz_ref.shape
    dz = dz_ref[...]
    edge = (dot(dz, wn_ref[...], 1, 1) / deg_ref[...]).astype(BF)
    other_ref[...] = dot(ct2_ref[...], edge).astype(BF)
    mine_ref[...] = dot(ct_ref[verts:, :], edge)
    base_ref[...] = dot(dz, ws_ref[...], 1, 1) + dot(ct_ref[:verts, :], edge)


def half_kernel(keep_ref, got_ref, out_ref):
    out_ref[...] = (keep_ref[...] + got_ref[...].astype(F32)).astype(BF).reshape(out_ref.shape)


def pair_kernel(mine_ref, got_ref, own_ref, s1_ref, s2_ref, s3_ref):
    x = lax.axis_index("x")
    for k, ref in enumerate((own_ref, s1_ref, s2_ref, s3_ref)):
        j = lax.rem(x + k, NX)
        ref[...] = (mine_ref[j] + got_ref[j].astype(F32)).astype(BF)


def join(a, b):
    return jnp.concatenate([a[:, :HUB], b[:, :HUB]], axis=1)


def packs(ref):
    return ref[...].astype(F32).reshape(-1, PACK, ref.shape[-1])


def pack_kernel(got_ref, own_ref, r1_ref, r2_ref, r3_ref, out_ref):
    rows = got_ref.shape[1]
    total = jnp.sum(got_ref[...].astype(F32), axis=0).astype(BF)
    out_ref[:, :rows, :] = jnp.broadcast_to(total[None], (NZ,) + total.shape)
    own, r1, r2, r3 = (packs(r) for r in (own_ref, r1_ref, r2_ref, r3_ref))
    k = iota(own.shape, 1)
    first = jnp.where(k < HUB, own, own + r1 + r2 + r3)
    out_ref[:, rows : rows + PACK, :] = first.astype(BF)
    out_ref[:, rows + PACK : rows + 2 * PACK, :] = join(r1, r2).astype(BF)
    out_ref[:, rows + 2 * PACK :, :] = join(r3, jnp.zeros_like(r3)).astype(BF)


def unpack_kernel(got_ref, out_ref, hub_ref):
    rows = out_ref.shape[1]
    total = jnp.sum(got_ref[:, :rows, :].astype(F32), axis=0).astype(BF)
    out_ref[...] = jnp.broadcast_to(total[None], out_ref.shape)
    hub_ref[...] = jnp.sum(got_ref[:, rows : rows + PACK, :].astype(F32), axis=0).astype(BF)


def grad_kernel(slot_ref, base_ref, sel_ref, got_ref, r1_ref, r2_ref, r3_ref, out_ref):
    verts, width = base_ref.shape
    x = lax.axis_index("x")
    rows = got_ref.shape[1] - 3 * PACK
    block = NZ * PACK
    own = sel_ref[x]
    b1, b2, b3 = (sel_ref[lax.rem(x - k + NX, NX)].astype(F32).reshape(NZ, PACK, verts) for k in (1, 2, 3))
    pair = join(b1, b2).reshape(block, verts).astype(BF)
    last = join(b3, jnp.zeros_like(b3)).reshape(block, verts).astype(BF)
    out = base_ref[...]
    for i, sel in enumerate((own, pair, last)):
        at = rows + i * PACK
        out = out + dot(sel, got_ref[:, at : at + PACK, :].reshape(block, width), 0, 0)
    hub = jnp.zeros((1, width), F32)
    for i, ref in ((3, r1_ref), (2, r2_ref), (1, r3_ref)):
        hub = hub + ref[...].astype(F32)[HUB + i : HUB + i + 1]
    out_ref[...] = out + jnp.where(iota((verts, width), 0) == slot_ref[0], hub, 0.0)


def weight_kernel(*refs, own):
    got_ref = refs[0]
    self_ref, neigh_ref, buf, sem = refs[1 if own else 3 :]
    _, c = place()
    half = got_ref.shape[0] // 2
    to_self = (c == 0) if own else (c != 0)

    def write(ref):
        copies = []
        for i in range(2):
            rows = pl.ds(i * half, half)
            buf[rows, :] = got_ref[rows, :].astype(F32)
            copy = pltpu.make_async_copy(buf.at[rows, :], ref.at[rows, :], sem.at[i])
            copy.start()
            copies.append(copy)
        for copy in copies:
            copy.wait()

    pl.when(to_self)(lambda: write(self_ref))
    pl.when(jnp.logical_not(to_self))(lambda: write(neigh_ref))


def swap_core(v):
    return lax.ppermute(v, "c", [(0, 1), (1, 0)])


def shift(v, axis, k):
    return lax.ppermute(v, axis, [(i, (i + k) % 4) for i in range(4)])


def exchange(v, axes):
    return lax.all_to_all(v, axes, split_axis=0, concat_axis=0, tiled=True)


def body(features, w_self, w_neigh, cotangent, neighbours, hub_slots, send_rows, send_counts):
    verts, width = features.shape
    peers, cap = send_rows.shape[1:]
    hubs = 256
    packed = peers * PACK
    table = verts + hubs + peers * cap
    rows = verts + packed

    hub_row = lax.dynamic_slice(features, (hub_slots[0].astype(jnp.uint32), jnp.uint32(0)), (1, width))
    hub_in = [shift(hub_row, "y", k) for k in (1, 2, 3)]
    ct, cm, degree, index = call(
        functools.partial(count_kernel, packed=packed, hubs=hubs, table=table),
        [((rows, verts), BF), ((verts, rows), BF), ((verts, 1), F32), (neighbours.shape[::-1], I32)],
        "count",
        flops=1 << 28,
    )(neighbours.T)
    hub_in, ct, cm = lax.optimization_barrier((hub_in, ct, cm))
    outgoing, sel = call(
        outgoing_kernel, [((peers, PACK, width), BF), ((packed, verts), BF)], "outgoing", smem=(0,)
    )(hub_slots, send_rows[0].T, send_counts, features, *hub_in)
    first = exchange(outgoing, ("x", "z"))
    first_other = swap_core(first)
    ct2, cm2, z_self, s_local = call(
        local_kernel,
        [((packed, verts), BF), ((verts, packed), BF), ((verts, width), F32), ((verts, width), F32)],
        "local",
    )(features, w_self, cm, index)

    hidden, dz, w_send, w_keep = call(
        forward_kernel,
        [((verts, width), BF), ((verts, width), BF), ((width, width), BF), ((width, width), F32)],
        "forward",
    )(features, cotangent, w_neigh, cm, cm2, degree, z_self, s_local, first, first_other)

    w_got = swap_core(w_send)
    base, mine, other = call(
        backward_kernel,
        [((verts, width), F32), ((packed, width), F32), ((packed, width), BF)],
        "backward",
    )(dz, w_neigh, w_self, degree, ct, ct2)

    part = width // (NY * NX)
    other_got = swap_core(other)
    w_keep, mine = lax.optimization_barrier((w_keep, mine))
    blocks = call(half_kernel, [((NY * NX, part, width), BF)], "half")(w_keep, w_got)[0]
    second = exchange(blocks, ("y", "x"))

    split = (NX, NZ * PACK, width)
    b_own, *b_out = call(pair_kernel, [(split[1:], BF)] * 4, "pair")(
        mine.reshape(split), other_got.reshape(split)
    )
    b_in = [shift(b_out[k - 1], "x", k) for k in (1, 2, 3)]
    pack = call(pack_kernel, [((NZ, part + 3 * PACK, width), BF)], "pack")(second, b_own, *b_in)[0]
    third = exchange(pack, "z")
    copies, hub = call(unpack_kernel, [((NY * NX, part, width), BF), ((PACK, width), BF)], "unpack")(third)
    fourth = exchange(copies, ("y", "x")).reshape(width, width)
    hub_back = [shift(hub, "y", k) for k in (1, 2, 3)]
    grad_features = call(grad_kernel, [((verts, width), F32)], "grad", smem=(0,))(
        hub_slots, base, sel.reshape(NX, NZ * PACK, verts), third, *hub_back
    )[0]
    fourth, grad_features = lax.optimization_barrier((fourth, grad_features))
    other = swap_core(fourth)
    scratch = (pltpu.VMEM((width, width), F32), pltpu.SemaphoreType.DMA((2,)))
    shapes = [((width, width), F32)] * 2
    partial = call(
        functools.partial(weight_kernel, own=True), shapes, "mine", hbm_out=True, scratch=scratch
    )(fourth)
    grad_self, grad_neigh = call(
        functools.partial(weight_kernel, own=False), shapes, "other", hbm=(1, 2), hbm_out=True, scratch=scratch,
        alias={1: 0, 2: 1},
    )(other, *partial)
    return (hidden, grad_features, grad_self, grad_neigh)


def solution(mesh):
    every = ("y", "c", "x", "z")
    fine = Mesh(mesh.devices.reshape(NY, 2, NX, NZ), every)
    vertex = P(every, None)
    return jax.shard_map(
        body,
        mesh=fine,
        in_specs=(vertex, P(), P(), vertex, vertex, P(every), P(every, None, None), vertex),
        out_specs=(vertex, vertex, P(), P()),
        check_vma=False,
    )
```

```python
import functools

import jax
import jax.numpy as jnp
from jax import lax
from jax.experimental import pallas as pl
from jax.experimental.pallas import tpu as pltpu
from jax.sharding import Mesh
from jax.sharding import PartitionSpec as P

BF = jnp.bfloat16
F32 = jnp.float32
I32 = jnp.int32
PACK = 8
HUB = 4
NY, NX, NZ = 4, 4, 8


def dot(a, b, ca=1, cb=0):
    return lax.dot_general(a, b, (((ca,), (cb,)), ((), ())), preferred_element_type=F32)


def call(kernel, outs, name, flops=1 << 22, nbytes=1 << 20, smem=(), hbm=(), hbm_out=False, scratch=(), alias=None):
    outs = [jax.ShapeDtypeStruct(s, d) for s, d in outs]
    vector = pl.BlockSpec(memory_space=pltpu.VMEM)
    scalar = pl.BlockSpec(memory_space=pltpu.SMEM)
    main = pl.BlockSpec(memory_space=pltpu.HBM)

    def run(*args):
        return pl.pallas_call(
            kernel,
            out_shape=outs,
            in_specs=[scalar if i in smem else main if i in hbm else vector for i in range(len(args))],
            out_specs=[main if hbm_out is True or (hbm_out and i in hbm_out) else vector for i in range(len(outs))],
            scratch_shapes=list(scratch),
            input_output_aliases=alias or {},
            name=name,
            compiler_params=pltpu.CompilerParams(vmem_limit_bytes=32 << 20),
            cost_estimate=pl.CostEstimate(flops=flops, bytes_accessed=nbytes, transcendentals=0),
        )(*args)

    return run


def place():
    return lax.axis_index("y"), lax.axis_index("c")


def iota(shape, dim):
    return lax.broadcasted_iota(I32, shape, dim)


def outgoing_kernel(slot_ref, route_ref, count_ref, feat_ref, r1_ref, r2_ref, r3_ref, out_ref, sel_ref):
    packed, verts = sel_ref.shape
    cap, peers = route_ref.shape
    live = iota((cap, peers), 0) < count_ref[...]
    routes = jnp.where(live, route_ref[...], -1).astype(F32).astype(BF)
    owner = (iota((packed, peers), 0) // PACK == iota((packed, peers), 1)).astype(BF)
    every = dot(owner, routes, 1, 1)
    k = lax.rem(iota((packed, cap), 0), PACK)
    pick = jnp.sum(jnp.where(k == iota((packed, cap), 1), every, 0.0), axis=1, keepdims=True).astype(I32)
    k = lax.rem(iota((packed, 1), 0), PACK)
    pick = jnp.where(k < cap, pick, jnp.where(k == HUB, slot_ref[0], -1))
    sel = (pick == iota((packed, verts), 1)).astype(BF)
    sel_ref[...] = sel
    rows = dot(sel, feat_ref[...])
    k = lax.rem(iota(rows.shape, 0), PACK)
    for i, ref in ((1, r1_ref), (2, r2_ref), (3, r3_ref)):
        rows = jnp.where(k == HUB + i, ref[...].astype(F32)[:1], rows)
    out_ref[...] = rows.astype(BF).reshape(out_ref.shape)


def packed_index(nb, verts, packed, hubs):
    y, c = place()
    h = nb - verts
    p, dom = lax.rem(h, 32), h // 32
    row = p * PACK + HUB + lax.rem(y - dom // 2 + NY, NY)
    hub = verts + row + jnp.where(lax.rem(dom, 2) == c, 0, packed)
    b = nb - verts - hubs
    bound = verts + (b // 4) * PACK + lax.rem(b, 4)
    far = jnp.where(nb < verts + hubs, hub, jnp.where(b < packed // 2, bound, -1))
    return jnp.where(nb < verts, nb, far)


def count_tile(index, at, step=128):
    slots, verts = index.shape
    index = jnp.clip(index - at, -1, step).astype(F32).astype(BF)
    rows = iota((step, verts), 0).astype(F32).astype(BF)
    one, zero = jnp.ones((), BF), jnp.zeros((), BF)
    acc = jnp.zeros((step, verts), BF)
    for j in range(slots):
        acc = acc + jnp.where(index[j : j + 1, :] == rows, one, zero)
    return acc


def count_kernel(nbt_ref, ct_ref, c_ref, deg_ref, index_ref, *, packed, hubs, table):
    verts = nbt_ref.shape[1]
    nbt = nbt_ref[...]
    degree = jnp.sum((nbt < table).astype(F32), axis=0, keepdims=True)
    deg_ref[...] = jnp.broadcast_to(degree, (8, verts)).T[:, :1]
    index = packed_index(nbt, verts, packed, hubs)
    index_ref[...] = index
    for t in range(0, verts + packed, 128):
        acc = count_tile(index, t)
        ct_ref[t : t + 128, :] = acc
        c_ref[:, t : t + 128] = acc.astype(F32).T.astype(BF)


def local_kernel(feat_ref, ws_ref, c_ref, index_ref, ct2_ref, c2_ref, zs_ref, s1_ref):
    feat = feat_ref[...]
    verts = feat.shape[0]
    zs_ref[...] = dot(feat, ws_ref[...])
    s1_ref[...] = dot(c_ref[:, :verts], feat)
    index = index_ref[...]
    for t in range(0, c2_ref.shape[1], 128):
        acc = count_tile(index, c_ref.shape[1] + t)
        ct2_ref[t : t + 128, :] = acc
        c2_ref[:, t : t + 128] = acc.astype(F32).T.astype(BF)


def forward_kernel(
    feat_ref, cot_ref, wn_ref, c_ref, c2_ref, deg_ref, zs_ref, s1_ref, got_ref, other_ref,
    hid_ref, dz_ref, send_ref, keep_ref,
):
    verts, width = feat_ref.shape
    _, c = place()
    got = got_ref[...].reshape(-1, width)
    other = other_ref[...].reshape(-1, width)
    sums = s1_ref[...] + dot(c_ref[:, verts:], got) + dot(c2_ref[...], other)
    agg = (sums / deg_ref[...]).astype(BF)
    z = zs_ref[...] + dot(agg, wn_ref[...])
    sig = jax.nn.sigmoid(z)
    hid_ref[...] = (z * sig).astype(BF)
    dz = (cot_ref[...].astype(F32) * sig * (1.0 + z * (1.0 - sig))).astype(BF)
    dz_ref[...] = dz
    feat = feat_ref[...]
    first = c == 0
    send_ref[...] = dot(jnp.where(first, agg, feat), dz, 0, 0).astype(BF)
    keep_ref[...] = dot(jnp.where(first, feat, agg), dz, 0, 0)


def backward_kernel(dz_ref, wn_ref, ws_ref, deg_ref, ct_ref, ct2_ref, base_ref, mine_ref, other_ref):
    verts, width = dz_ref.shape
    dz = dz_ref[...]
    edge = (dot(dz, wn_ref[...], 1, 1) / deg_ref[...]).astype(BF)
    other_ref[...] = dot(ct2_ref[...], edge).astype(BF)
    mine_ref[...] = dot(ct_ref[verts:, :], edge)
    base_ref[...] = dot(dz, ws_ref[...], 1, 1) + dot(ct_ref[:verts, :], edge)


def half_kernel(keep_ref, got_ref, out_ref, buf, sem):
    blocks, part, _ = buf.shape
    step = blocks // 4
    copies = []
    for i in range(4):
        rows = slice(i * step * part, (i + 1) * step * part)
        total = (keep_ref[rows, :] + got_ref[rows, :].astype(F32)).astype(BF)
        span = pl.ds(i * step, step)
        buf[span] = total.reshape(step, part, total.shape[1])
        copy = pltpu.make_async_copy(buf.at[span], out_ref.at[span], sem.at[i])
        copy.start()
        copies.append(copy)
    for copy in copies:
        copy.wait()


def pair_kernel(mine_ref, got_ref, own_ref, s1_ref, s2_ref, s3_ref):
    x = lax.axis_index("x")
    for k, ref in enumerate((own_ref, s1_ref, s2_ref, s3_ref)):
        j = lax.rem(x + k, NX)
        ref[...] = (mine_ref[j] + got_ref[j].astype(F32)).astype(BF)


def join(a, b):
    return jnp.concatenate([a[:, :HUB], b[:, :HUB]], axis=1)


def packs(ref):
    return ref[...].astype(F32).reshape(-1, PACK, ref.shape[-1])


def pack_kernel(got_ref, own_ref, r1_ref, r2_ref, r3_ref, out_ref):
    rows = got_ref.shape[1]
    total = jnp.sum(got_ref[...].astype(F32), axis=0).astype(BF)
    out_ref[:, :rows, :] = jnp.broadcast_to(total[None], (NZ,) + total.shape)
    own, r1, r2, r3 = (packs(r) for r in (own_ref, r1_ref, r2_ref, r3_ref))
    k = iota(own.shape, 1)
    first = jnp.where(k < HUB, own, own + r1 + r2 + r3)
    out_ref[:, rows : rows + PACK, :] = first.astype(BF)
    out_ref[:, rows + PACK : rows + 2 * PACK, :] = join(r1, r2).astype(BF)
    out_ref[:, rows + 2 * PACK :, :] = join(r3, jnp.zeros_like(r3)).astype(BF)


def unpack_kernel(got_ref, out_ref, hub_ref, buf, sem):
    rows = buf.shape[0]
    buf[...] = jnp.sum(got_ref[:, :rows, :].astype(F32), axis=0).astype(BF)
    copies = [pltpu.make_async_copy(buf, out_ref.at[i], sem.at[i]) for i in range(out_ref.shape[0])]
    for copy in copies:
        copy.start()
    hub_ref[...] = jnp.sum(got_ref[:, rows : rows + PACK, :].astype(F32), axis=0).astype(BF)
    for copy in copies:
        copy.wait()


def grad_kernel(slot_ref, base_ref, sel_ref, got_ref, r1_ref, r2_ref, r3_ref, out_ref):
    verts, width = base_ref.shape
    x = lax.axis_index("x")
    rows = got_ref.shape[1] - 3 * PACK
    block = NZ * PACK
    own = sel_ref[x]
    b1, b2, b3 = (sel_ref[lax.rem(x - k + NX, NX)].astype(F32).reshape(NZ, PACK, verts) for k in (1, 2, 3))
    pair = join(b1, b2).reshape(block, verts).astype(BF)
    last = join(b3, jnp.zeros_like(b3)).reshape(block, verts).astype(BF)
    out = base_ref[...]
    for i, sel in enumerate((own, pair, last)):
        at = rows + i * PACK
        out = out + dot(sel, got_ref[:, at : at + PACK, :].reshape(block, width), 0, 0)
    hub = jnp.zeros((1, width), F32)
    for i, ref in ((3, r1_ref), (2, r2_ref), (1, r3_ref)):
        hub = hub + ref[...].astype(F32)[HUB + i : HUB + i + 1]
    out_ref[...] = out + jnp.where(iota((verts, width), 0) == slot_ref[0], hub, 0.0)


def weight_kernel(*refs, own):
    got_ref = refs[0]
    self_ref, neigh_ref, buf, sem = refs[1 if own else 3 :]
    _, c = place()
    half = got_ref.shape[0] // 2
    to_self = (c == 0) if own else (c != 0)

    def write(ref):
        copies = []
        for i in range(2):
            rows = pl.ds(i * half, half)
            buf[rows, :] = got_ref[rows, :].astype(F32)
            copy = pltpu.make_async_copy(buf.at[rows, :], ref.at[rows, :], sem.at[i])
            copy.start()
            copies.append(copy)
        for copy in copies:
            copy.wait()

    pl.when(to_self)(lambda: write(self_ref))
    pl.when(jnp.logical_not(to_self))(lambda: write(neigh_ref))


def swap_core(v):
    return lax.ppermute(v, "c", [(0, 1), (1, 0)])


def shift(v, axis, k):
    return lax.ppermute(v, axis, [(i, (i + k) % 4) for i in range(4)])


def exchange(v, axes):
    return lax.all_to_all(v, axes, split_axis=0, concat_axis=0, tiled=True)


def body(features, w_self, w_neigh, cotangent, neighbours, hub_slots, send_rows, send_counts):
    verts, width = features.shape
    peers, cap = send_rows.shape[1:]
    hubs = 256
    packed = peers * PACK
    table = verts + hubs + peers * cap
    rows = verts + packed

    hub_row = lax.dynamic_slice(features, (hub_slots[0].astype(jnp.uint32), jnp.uint32(0)), (1, width))
    hub_in = [shift(hub_row, "y", k) for k in (1, 2, 3)]
    ct, cm, degree, index = call(
        functools.partial(count_kernel, packed=packed, hubs=hubs, table=table),
        [((rows, verts), BF), ((verts, rows), BF), ((verts, 1), F32), (neighbours.shape[::-1], I32)],
        "count",
        flops=1 << 28,
    )(neighbours.T)
    hub_in, ct, cm = lax.optimization_barrier((hub_in, ct, cm))
    outgoing, sel = call(
        outgoing_kernel, [((peers, PACK, width), BF), ((packed, verts), BF)], "outgoing", smem=(0,)
    )(hub_slots, send_rows[0].T, send_counts, features, *hub_in)
    first = exchange(outgoing, ("x", "z"))
    first_other = swap_core(first)
    ct2, cm2, z_self, s_local = call(
        local_kernel,
        [((packed, verts), BF), ((verts, packed), BF), ((verts, width), F32), ((verts, width), F32)],
        "local",
    )(features, w_self, cm, index)

    hidden, dz, w_send, w_keep = call(
        forward_kernel,
        [((verts, width), BF), ((verts, width), BF), ((width, width), BF), ((width, width), F32)],
        "forward",
    )(features, cotangent, w_neigh, cm, cm2, degree, z_self, s_local, first, first_other)

    w_got = swap_core(w_send)
    base, mine, other = call(
        backward_kernel,
        [((verts, width), F32), ((packed, width), F32), ((packed, width), BF)],
        "backward",
    )(dz, w_neigh, w_self, degree, ct, ct2)

    part = width // (NY * NX)
    other_got = swap_core(other)
    w_keep, mine = lax.optimization_barrier((w_keep, mine))
    blocks = call(half_kernel, [((NY * NX, part, width), BF)], "half", hbm_out=True,
        scratch=(pltpu.VMEM((NY * NX, part, width), BF), pltpu.SemaphoreType.DMA((4,))),
    )(w_keep, w_got)[0]
    second = exchange(blocks, ("y", "x"))

    split = (NX, NZ * PACK, width)
    b_own, *b_out = call(pair_kernel, [(split[1:], BF)] * 4, "pair")(
        mine.reshape(split), other_got.reshape(split)
    )
    b_in = [shift(b_out[k - 1], "x", k) for k in (1, 2, 3)]
    pack = call(pack_kernel, [((NZ, part + 3 * PACK, width), BF)], "pack")(second, b_own, *b_in)[0]
    third = exchange(pack, "z")
    copies, hub = call(unpack_kernel, [((NY * NX, part, width), BF), ((PACK, width), BF)], "unpack", hbm_out=(0,),
        scratch=(pltpu.VMEM((part, width), BF), pltpu.SemaphoreType.DMA((NY * NX,))),
    )(third)
    fourth = exchange(copies, ("y", "x")).reshape(width, width)
    hub_back = [shift(hub, "y", k) for k in (1, 2, 3)]
    grad_features = call(grad_kernel, [((verts, width), F32)], "grad", smem=(0,))(
        hub_slots, base, sel.reshape(NX, NZ * PACK, verts), third, *hub_back
    )[0]
    fourth, grad_features = lax.optimization_barrier((fourth, grad_features))
    other = swap_core(fourth)
    scratch = (pltpu.VMEM((width, width), F32), pltpu.SemaphoreType.DMA((2,)))
    shapes = [((width, width), F32)] * 2
    partial = call(
        functools.partial(weight_kernel, own=True), shapes, "mine", hbm_out=True, scratch=scratch
    )(fourth)
    grad_self, grad_neigh = call(
        functools.partial(weight_kernel, own=False), shapes, "other", hbm=(1, 2), hbm_out=True, scratch=scratch,
        alias={1: 0, 2: 1},
    )(other, *partial)
    return (hidden, grad_features, grad_self, grad_neigh)


def solution(mesh):
    every = ("y", "c", "x", "z")
    fine = Mesh(mesh.devices.reshape(NY, 2, NX, NZ), every)
    vertex = P(every, None)
    return jax.shard_map(
        body,
        mesh=fine,
        in_specs=(vertex, P(), P(), vertex, vertex, P(every), P(every, None, None), vertex),
        out_specs=(vertex, vertex, P(), P()),
        check_vma=False,
    )
```
